32 devices in a mesh: freq: 2 (over y), col: 4 (over z), row: 2 (over x), help: 2 (over core).
Axes of the slice: x: 2, y: 2, z: 4, core: 2. Of those that a mesh axis runs over, the one named last changes fastest.
Arguments:
- wavefield: bfloat16 [4, 64, 512, 128], P('freq', 'col', ('row', 'help')), parts along dimension 0, may hold values from -6 to 6
- basis_factor: bfloat16 [4, 8, 64, 80, 512], P('freq', 'row', 'col', 'help'), parts along dimension 0, may hold values from -0.0625 to 0.0625
- second_factor: bfloat16 [4, 8, 64, 80, 512], P('freq', 'row', 'col', 'help'), parts along dimension 0, may hold values from -0.1875 to 0.1875
- tile_ranks: int32 [16, 64], P(('freq', 'row'), 'col'), parts along dimension 0, may hold values from 16 to 80
- observed: bfloat16 [4, 8, 512, 128], P('freq', 'row', ('col', 'help')), parts along dimension 0, may hold values from -6 to 6
- amplitude: bfloat16 [16, 512, 128], P(('freq', 'row'), ('col', 'help')), parts along dimension 0, may hold values from 0.29882812 to 3
Outputs:
- residual: bfloat16 [4, 8, 512, 128], P('freq', 'row', ('col', 'help')), parts along dimension 0
- adjoint: bfloat16 [4, 64, 512, 128], P('freq', 'col', ('row', 'help')), parts along dimension 0
The draws below stay inside these ranges and needn't reach their ends.
There are 2 independent parts, one for each index of `freq`. The reference program is written for one: setup_inputs(seed, part) draws one part's arguments, and reference() takes and returns one part's arrays. A program takes and returns all parts, laid end to end along the dimension named above; each array names one. Nothing has to cross between parts.
Inputs may be any that keep to these rules, and one draw needn't show every extreme that they name: `tile_ranks`: entries of a tile's factors at rank terms from its rank on are not part of the kernel.
All inputs are finite; a program needn't handle non-finite values.
Results may differ from the reference program's by a relative error of at most 0.006.
Values may be sent and summed in bfloat16 or wider, within the bound.
A program may use at most 128 MiB of HBM per device.

```python
import math
import jax
import jax.numpy as jnp
from jax import lax

TILE = 512
RMAX = 80
RMIN = 16
RHS = 128
TC = 64
TR = 8


def plant(array, rng, low, high):
    dims = array.shape
    index_at = [jax.random.randint(jax.random.fold_in(rng, axis), (), 0, dims[axis]) for axis in range(len(dims))]
    array = array.at[tuple(index_at)].set(low)
    longest = dims.index(max(dims))
    index_at[longest] = (index_at[longest] + 1) % dims[longest]
    return array.at[tuple(index_at)].set(high)


def level_of(stream_key, extent, cuts, low, top_value):
    gain = 1.0
    for position, parts in cuts:
        draws = jax.random.uniform(jax.random.fold_in(jax.random.fold_in(stream_key, 6), position), (parts,), jnp.float32, low / len(cuts), top_value / len(cuts))
        gain = gain * jnp.repeat(jnp.exp(draws), extent[position] // parts).reshape((-1,) + (1,) * (len(extent) - 1 - position))
    return gain


def normal_values(rng, extent, scale, limit, split=(), kind=jnp.bfloat16):
    entries = scale * jax.random.normal(rng, extent, jnp.float32)
    if split:
        entries = entries * level_of(rng, extent, split, -0.22, 0.18)
    return jnp.clip(entries, -limit, limit).astype(kind)


def setup_inputs(seed: int = 0, part: int = 0) -> dict:
    splits = jax.random.split(jax.random.key(seed), 7)
    part_splits = jax.random.split(jax.random.fold_in(splits[6], part), 7)
    wavefield = normal_values(part_splits[0], (2, TC, TILE, RHS), 1.0, 6.0, ((1, 4), (2, 4)))
    basis_factor = normal_values(part_splits[1], (2, TR, TC, RMAX, TILE), (2 * TC * RMAX) ** -0.5, 0.0625, ((1, 2), (2, 4), (3, 2)))
    second_factor = normal_values(part_splits[2], (2, TR, TC, RMAX, TILE), (2 * TILE) ** -0.5, 0.1875, ((1, 2), (2, 4), (3, 2)))
    tile_ranks = plant(jax.random.randint(part_splits[3], (TR, TC), RMIN, RMAX + 1), jax.random.fold_in(part_splits[3], 1), RMIN, RMAX).astype(jnp.int32)
    observed = normal_values(part_splits[4], (2, TR, TILE, RHS), 1.0, 6.0, ((1, 2), (2, 8)))
    amplitude = jnp.clip(jnp.exp(math.log(3.0) - 2.306499 * jax.random.uniform(part_splits[5], (TR, TILE, RHS), jnp.float32) ** level_of(part_splits[5], (TR, TILE, RHS), ((0, 2), (1, 8)), -0.2, 0.2)), 0.29882812, 3.0).astype(jnp.bfloat16)
    return dict(wavefield=wavefield, basis_factor=basis_factor, second_factor=second_factor, tile_ranks=tile_ranks, observed=observed, amplitude=amplitude)


def settle(value):
    return lax.optimization_barrier(value.astype(jnp.bfloat16)).astype(jnp.float32)


def tile_row(basis_row, second_row, rank_row, waves, observed_row, amplitude_row):
    basis_row = basis_row.astype(jnp.float32)
    second_row = second_row.astype(jnp.float32)
    terms = jnp.arange(RMAX, dtype=jnp.int32)
    keep = (terms[None, :] < rank_row[:, None]).astype(jnp.float32)[:, :, None]
    coef_real = jnp.einsum('pjkt,pjtn->jkn', second_row, waves)
    coef_imag = jnp.einsum('jkt,jtn->jkn', second_row[0], waves[1]) - jnp.einsum('jkt,jtn->jkn', second_row[1], waves[0])
    coef_real = settle(coef_real * keep)
    coef_imag = settle(coef_imag * keep)
    forward_real = jnp.einsum('jks,jkn->sn', basis_row[0], coef_real) - jnp.einsum('jks,jkn->sn', basis_row[1], coef_imag)
    forward_imag = jnp.einsum('jks,jkn->sn', basis_row[0], coef_imag) + jnp.einsum('jks,jkn->sn', basis_row[1], coef_real)
    forward = jnp.stack([forward_real, forward_imag])
    weight = amplitude_row.astype(jnp.float32)[None]
    residual_row = (weight * (forward - observed_row.astype(jnp.float32))).astype(jnp.bfloat16)
    resid = residual_row.astype(jnp.float32)
    back_real = jnp.einsum('pjks,psn->jkn', basis_row, resid)
    back_imag = jnp.einsum('jks,sn->jkn', basis_row[0], resid[1]) - jnp.einsum('jks,sn->jkn', basis_row[1], resid[0])
    back_real = settle(back_real * keep)
    back_imag = settle(back_imag * keep)
    adjoint_real = jnp.einsum('jkt,jkn->jtn', second_row[0], back_real) - jnp.einsum('jkt,jkn->jtn', second_row[1], back_imag)
    adjoint_imag = jnp.einsum('jkt,jkn->jtn', second_row[0], back_imag) + jnp.einsum('jkt,jkn->jtn', second_row[1], back_real)
    return residual_row, jnp.stack([adjoint_real, adjoint_imag])


def reference(wavefield, basis_factor, second_factor, tile_ranks, observed, amplitude):
    waves = wavefield.astype(jnp.float32)

    def step(carry, index):
        basis_row = lax.dynamic_index_in_dim(basis_factor, index, 1, keepdims=False)
        second_row = lax.dynamic_index_in_dim(second_factor, index, 1, keepdims=False)
        rank_row = lax.dynamic_index_in_dim(tile_ranks, index, 0, keepdims=False)
        observed_row = lax.dynamic_index_in_dim(observed, index, 1, keepdims=False)
        amplitude_row = lax.dynamic_index_in_dim(amplitude, index, 0, keepdims=False)
        residual_row, term = tile_row(basis_row, second_row, rank_row, waves, observed_row, amplitude_row)
        return carry + term, residual_row

    start = jnp.zeros((2, TC, TILE, RHS), jnp.float32)
    total, residual_rows = lax.scan(step, start, jnp.arange(TR, dtype=jnp.int32))
    residual = jnp.moveaxis(residual_rows, 0, 1)
    return residual, total.astype(jnp.bfloat16)
```

```python
import functools

import jax
import jax.numpy as jnp
from jax import lax
from jax.experimental import pallas as pl
from jax.experimental.pallas import tpu as pltpu
from jax.sharding import PartitionSpec as P

MESH = pl.DeviceIdType.MESH
BF, F32 = jnp.bfloat16, jnp.float32


def loop(n, f):
    def step(i, carry):
        f(i)
        return carry

    lax.fori_loop(0, n, step, 0)


def mul_t(lhs, rhs):
    return lax.dot_general(lhs, rhs, (((0,), (0,)), ((), ())), preferred_element_type=F32)


def kernel(R, C, JC, x, u, v, ranks, obs, amp, res_o, adj_o,
           us, vs, xs, cf, ft, fo, fss, fsr, zs, zr, rs, at, ao, ass, asr, gs, gr,
           u_sem, v_sem, loc_sem, xg_s, xg_r, xf_s, xf_r, fs_s, fs_r, z_s, z_r,
           rg_s, rg_r, rf_s, rf_r, as_s, as_r, ag_s, ag_r):
    _, J, TB, N = x.shape
    I, SB = obs.shape[1], obs.shape[2]
    K = v.shape[3]
    IK, JK = I * K, J * K
    NC = J // JC
    r, c, h = lax.axis_index("row"), lax.axis_index("col"), lax.axis_index("help")
    sib = {"help": 1 - h}

    def row(d):
        return lax.rem(r + d, R)

    def col(d):
        return lax.rem(c + d, C)

    def tds(r2, h2):
        return pl.ds(pl.multiple_of((r2 * 2 + h2) * TB, TB), TB)

    def sds(c2, h2):
        return pl.ds(pl.multiple_of((c2 * 2 + h2) * SB, SB), SB)

    def sblk(c2):
        return pl.ds(pl.multiple_of(c2 * SB, SB), SB)

    def tblk(r2):
        return pl.ds(pl.multiple_of(r2 * TB, TB), TB)

    def jds(q):
        return pl.ds(q * JC, JC)

    def rc(src, dst, s, rr, dev):
        return pltpu.make_async_remote_copy(
            src_ref=src, dst_ref=dst, send_sem=s, recv_sem=rr, device_id=dev, device_id_type=MESH)

    def load_v(j):
        for p in range(2):
            for i in range(I):
                pltpu.make_async_copy(
                    v.at[p, i, j], vs.at[j, pl.ds((p * I + i) * K, K)], v_sem.at[j]).start()

    loop(J, load_v)
    for i in range(I):
        for p in range(2):
            pltpu.make_async_copy(u.at[p * I + i], us.at[i, pl.ds(p * JK, JK)], u_sem.at[i]).start()
    own = pltpu.make_async_copy(x, xs.at[:, :, tds(r, h)], loc_sem.at[0])
    own.start()

    barrier = pltpu.get_barrier_semaphore()
    for d in range(1, R):
        pl.semaphore_signal(barrier, inc=1, device_id={"row": row(d)}, device_id_type=MESH)
    for d in range(1, C):
        pl.semaphore_signal(barrier, inc=1, device_id={"col": col(d)}, device_id_type=MESH)
    pl.semaphore_signal(barrier, inc=1, device_id=sib, device_id_type=MESH)
    pl.semaphore_wait(barrier, R + C - 1)

    def xg(q, r2):
        return rc(x.at[:, jds(q)], xs.at[:, jds(q), tds(r, h)], xg_s.at[q, r2], xg_r.at[q, r], {"row": r2})

    def xg_in(q, r2):
        reg = xs.at[:, jds(q), tds(r2, h)]
        return rc(reg, reg, xg_s.at[q, r2], xg_r.at[q, r2], {"row": r2})

    def xf(q, r2):
        reg = xs.at[:, jds(q), tds(r2, h)]
        return rc(reg, reg, xf_s.at[q, r2], xf_r.at[q, r2], sib)

    def xf_own(q):
        return rc(x.at[:, jds(q)], xs.at[:, jds(q), tds(r, h)], xf_s.at[q, r], xf_r.at[q, r], sib)

    def xf_in(q, r2):
        reg = xs.at[:, jds(q), tds(r2, 1 - h)]
        return rc(reg, reg, xf_s.at[q, r2], xf_r.at[q, r2], sib)

    def send_x(q):
        for d in range(1, R):
            xg(q, row(d)).start()
        xf_own(q).start()

    loop(NC, send_x)
    own.wait()

    kio = lax.broadcasted_iota(jnp.int32, (K, 2 * N), 0) + h * K

    def keep(i, j, value):
        return jnp.where(kio < ranks[i, j], value, 0.0)

    def coef(j):
        pltpu.make_async_copy(vs.at[j], vs.at[j], v_sem.at[j]).wait()
        xj = jnp.concatenate([xs[0, j], xs[1, j]], axis=1)
        m = jnp.dot(vs[j], xj, preferred_element_type=F32)
        a, b = m[:IK], m[IK:]
        y = jnp.concatenate([a[:, :N] + b[:, N:], a[:, N:] - b[:, :N]], axis=1)
        for i in range(I):
            cf[i, pl.ds(pl.multiple_of(j * K, 8), K)] = keep(i, j, y[i * K:(i + 1) * K])

    def step1(q):
        @pl.when(q < NC)
        def _():
            for d in range(1, R):
                xg_in(q, row(d)).wait_recv()
                xf(q, row(d)).start()

        @pl.when(q >= 1)
        def _():
            for r2 in range(R):
                xf_in(q - 1, r2).wait_recv()
            loop(JC, lambda jj: coef((q - 1) * JC + jj))

    loop(NC + 1, step1)

    def pair(y):
        y = y.astype(BF)
        return jnp.concatenate([y, jnp.concatenate([-y[:, N:], y[:, :N]], axis=1)], axis=0)

    def fs(i):
        return rc(fss.at[i], fsr.at[i], fs_s.at[i], fs_r.at[i], sib)

    def zc(i, c2):
        return rc(zs.at[i, c2], zr.at[i, c], z_s.at[i, c2], z_r.at[i, c], {"col": c2})

    def zc_in(i, c2):
        return rc(zs.at[i, c2], zr.at[i, c2], z_s.at[i, c2], z_r.at[i, c2], {"col": c2})

    def zstage(i):
        fs(i).wait_recv()
        for d in range(1, C):
            c2 = col(d)
            zs[i, c2] = (fo[i, sblk(c2)] + fsr[i, sblk(c2)].astype(F32)).astype(BF)
            zc(i, c2).start()

    def step2(i):
        @pl.when(i < I)
        def _():
            pltpu.make_async_copy(us.at[i], us.at[i], u_sem.at[i]).wait()
            ft[...] = mul_t(us[i], pair(cf[i]))
            for c2 in range(C):
                fo[i, pl.ds(c2 * SB, SB)] = ft[sds(c2, h)]
                fss[i, pl.ds(c2 * SB, SB)] = ft[sds(c2, 1 - h)].astype(BF)
            fs(i).start()

        @pl.when(i >= 1)
        def _():
            zstage(i - 1)

    loop(I + 1, step2)

    def rg(i, c2):
        reg = rs.at[i, sds(c, h)]
        return rc(reg, reg, rg_s.at[i, c2], rg_r.at[i, c], {"col": c2})

    def rg_in(i, c2):
        reg = rs.at[i, sds(c2, h)]
        return rc(reg, reg, rg_s.at[i, c2], rg_r.at[i, c2], {"col": c2})

    def rf(i, c2):
        reg = rs.at[i, sds(c2, h)]
        return rc(reg, reg, rf_s.at[i, c2], rf_r.at[i, c2], sib)

    def rf_in(i, c2):
        reg = rs.at[i, sds(c2, 1 - h)]
        return rc(reg, reg, rf_s.at[i, c2], rf_r.at[i, c2], sib)

    def step3(i):
        @pl.when(i < I)
        def _():
            tot = fo[i, sblk(c)] + fsr[i, sblk(c)].astype(F32)
            for d in range(1, C):
                zc_in(i, col(d)).wait_recv()
                tot = tot + zr[i, col(d)].astype(F32)
            w = amp[i].astype(F32)
            re = (w * (tot[:, :N] - obs[0, i].astype(F32))).astype(BF)
            im = (w * (tot[:, N:] - obs[1, i].astype(F32))).astype(BF)
            res_o[0, i] = re
            res_o[1, i] = im
            rs[i, sds(c, h)] = jnp.concatenate([re, im], axis=1)
            for d in range(1, C):
                rg(i, col(d)).start()
            rf(i, c).start()

        @pl.when(i >= 1)
        def _():
            for d in range(1, C):
                rg_in(i - 1, col(d)).wait_recv()
                rf(i - 1, col(d)).start()

    loop(I + 1, step3)

    def back(i):
        for c2 in range(C):
            rf_in(i, c2).wait_recv()
        m = jnp.dot(us[i], rs[i], preferred_element_type=F32)
        a, b = m[:JK], m[JK:]
        cf[i] = jnp.concatenate([a[:, :N] + b[:, N:], a[:, N:] - b[:, :N]], axis=1)

    loop(I, back)

    def asx(q):
        return rc(ass.at[jds(q)], asr.at[jds(q)], as_s.at[q], as_r.at[q], sib)

    def ag(q, r2):
        return rc(gs.at[q, r2], gr.at[q, r], ag_s.at[q, r2], ag_r.at[q, r], {"row": r2})

    def ag_in(q, r2):
        return rc(gs.at[q, r2], gr.at[q, r2], ag_s.at[q, r2], ag_r.at[q, r2], {"row": r2})

    def adjoint(j):
        y = jnp.concatenate(
            [keep(i, j, cf[i, pl.ds(pl.multiple_of(j * K, 8), K)]) for i in range(I)], axis=0)
        at[...] = mul_t(vs[j], pair(y))
        for r2 in range(R):
            ao[j, pl.ds(r2 * TB, TB)] = at[tds(r2, h)]
            ass[j, pl.ds(r2 * TB, TB)] = at[tds(r2, 1 - h)].astype(BF)

    def step4(q):
        @pl.when(q < NC)
        def _():
            loop(JC, lambda jj: adjoint(q * JC + jj))
            asx(q).start()

        @pl.when(q >= 1)
        def _():
            p = q - 1
            asx(p).wait_recv()
            for d in range(1, R):
                r2 = row(d)
                gs[p, r2] = (ao[jds(p), tblk(r2)] + asr[jds(p), tblk(r2)].astype(F32)).astype(BF)
                ag(p, r2).start()

    loop(NC + 1, step4)

    def final(q):
        tot = ao[jds(q), tblk(r)] + asr[jds(q), tblk(r)].astype(F32)
        for d in range(1, R):
            ag_in(q, row(d)).wait_recv()
            tot = tot + gr[q, row(d)].astype(F32)
        adj_o[0, jds(q)] = tot[:, :, :N].astype(BF)
        adj_o[1, jds(q)] = tot[:, :, N:].astype(BF)

    loop(NC, final)

    def drain_q(q):
        for d in range(1, R):
            xg(q, row(d)).wait_send()
            xf(q, row(d)).wait_send()
            ag(q, row(d)).wait_send()
        xf_own(q).wait_send()
        asx(q).wait_send()

    loop(NC, drain_q)

    def drain_i(i):
        fs(i).wait_send()
        rf(i, c).wait_send()
        for d in range(1, C):
            zc(i, col(d)).wait_send()
            rg(i, col(d)).wait_send()
            rf(i, col(d)).wait_send()

    loop(I, drain_i)


def body(R, C, wavefield, basis_factor, second_factor, tile_ranks, observed, amplitude):
    _, J, TB, N = wavefield.shape
    _, I, _, K, S = basis_factor.shape
    T = second_factor.shape[4]
    SB = observed.shape[2]
    JC = 2 if J % 2 == 0 else 1
    NC = J // JC
    vm = pltpu.VMEM
    dma = pltpu.SemaphoreType.DMA
    anys = pl.BlockSpec(memory_space=pl.ANY)
    vmem = pl.BlockSpec(memory_space=pltpu.VMEM)
    smem = pl.BlockSpec(memory_space=pltpu.SMEM)
    u = basis_factor.reshape(2 * I, J * K, S)
    return pl.pallas_call(
        functools.partial(kernel, R, C, JC),
        out_shape=(
            jax.ShapeDtypeStruct((2, I, SB, N), BF),
            jax.ShapeDtypeStruct((2, J, TB, N), BF),
        ),
        in_specs=[anys, anys, anys, smem, vmem, vmem],
        out_specs=(vmem, vmem),
        scratch_shapes=[
            vm((I, 2 * J * K, S), BF),
            vm((J, 2 * I * K, T), BF),
            vm((2, J, T, N), BF),
            vm((I, J * K, 2 * N), F32),
            vm((S, 2 * N), F32),
            vm((I, C * SB, 2 * N), F32),
            vm((I, C * SB, 2 * N), BF),
            vm((I, C * SB, 2 * N), BF),
            vm((I, C, SB, 2 * N), BF),
            vm((I, C, SB, 2 * N), BF),
            vm((I, S, 2 * N), BF),
            vm((T, 2 * N), F32),
            vm((J, R * TB, 2 * N), F32),
            vm((J, R * TB, 2 * N), BF),
            vm((J, R * TB, 2 * N), BF),
            vm((NC, R, JC, TB, 2 * N), BF),
            vm((NC, R, JC, TB, 2 * N), BF),
            dma((I,)), dma((J,)), dma((1,)),
            dma((NC, R)), dma((NC, R)), dma((NC, R)), dma((NC, R)),
            dma((I,)), dma((I,)), dma((I, C)), dma((I, C)),
            dma((I, C)), dma((I, C)), dma((I, C)), dma((I, C)),
            dma((NC,)), dma((NC,)), dma((NC, R)), dma((NC, R)),
        ],
        compiler_params=pltpu.CompilerParams(
            collective_id=0, has_side_effects=True, vmem_limit_bytes=60 * 1024 * 1024),
        name="mdc",
    )(wavefield, u, second_factor, tile_ranks, observed, amplitude)


def solution(mesh):
    return jax.shard_map(
        functools.partial(body, mesh.shape["row"], mesh.shape["col"]),
        mesh=mesh,
        in_specs=(
            P("freq", "col", ("row", "help"), None),
            P("freq", "row", "col", "help", None),
            P("freq", "row", "col", "help", None),
            P(("freq", "row"), "col"),
            P("freq", "row", ("col", "help"), None),
            P(("freq", "row"), ("col", "help"), None),
        ),
        out_specs=(
            P("freq", "row", ("col", "help"), None),
            P("freq", "col", ("row", "help"), None),
        ),
        check_vma=False,
    )
```

```python
import functools

import jax
import jax.numpy as jnp
from jax import lax
from jax.experimental import pallas as pl
from jax.experimental.pallas import tpu as pltpu
from jax.sharding import PartitionSpec as P

MESH = pl.DeviceIdType.MESH
BF, F32 = jnp.bfloat16, jnp.float32


def loop(n, f):
    def step(i, carry):
        f(i)
        return carry

    lax.fori_loop(0, n, step, 0)


def mul_t(lhs, rhs):
    return lax.dot_general(lhs, rhs, (((0,), (0,)), ((), ())), preferred_element_type=F32)


def kernel(R, C, JC, x, u, v, ranks, obs, amp, res_o, adj_o,
           us, vs, xin, xs, cf, ft, fo, fss, fsr, zs, zr, rs, at, ao, ass, asr, gs, gr,
           u_sem, v_sem, x_sem, xg_s, xg_r, xf_s, xf_r, fs_s, fs_r, z_s, z_r,
           rg_s, rg_r, rf_s, rf_r, as_s, as_r, ag_s, ag_r):
    _, J, TB, N = x.shape
    I, SB = obs.shape[1], obs.shape[2]
    K = v.shape[3]
    IK, JK = I * K, J * K
    NC = J // JC
    n = N // 2
    r, c, h = lax.axis_index("row"), lax.axis_index("col"), lax.axis_index("help")
    sib = {"help": 1 - h}

    def row(d):
        return lax.rem(r + d, R)

    def col(d):
        return lax.rem(c + d, C)

    def tds(r2, h2):
        return pl.ds(pl.multiple_of((r2 * 2 + h2) * TB, TB), TB)

    def sds(c2, h2):
        return pl.ds(pl.multiple_of((c2 * 2 + h2) * SB, SB), SB)

    def sblk(c2):
        return pl.ds(pl.multiple_of(c2 * SB, SB), SB)

    def tblk(r2):
        return pl.ds(pl.multiple_of(r2 * TB, TB), TB)

    def jds(q):
        return pl.ds(q * JC, JC)

    def rc(src, dst, s, rr, dev):
        return pltpu.make_async_remote_copy(
            src_ref=src, dst_ref=dst, send_sem=s, recv_sem=rr, device_id=dev, device_id_type=MESH)

    def swap(y):
        return pltpu.roll(y, n, y.ndim - 1)

    def low(y):
        return lax.broadcasted_iota(jnp.int32, y.shape, y.ndim - 1) < n

    def split(e, a, b):
        return jnp.where(low(a), a, swap(b)) if e == 0 else jnp.where(low(a), swap(a), b)

    def turn(y):
        z = swap(y)
        return jnp.where(low(y), z, -z)

    def x_load(q):
        return pltpu.make_async_copy(x.at[:, jds(q)], xin.at[:, jds(q)], x_sem.at[q])

    loop(NC, lambda q: x_load(q).start())

    barrier = pltpu.get_barrier_semaphore()
    for d in range(1, R):
        pl.semaphore_signal(barrier, inc=1, device_id={"row": row(d)}, device_id_type=MESH)
    for d in range(1, C):
        pl.semaphore_signal(barrier, inc=1, device_id={"col": col(d)}, device_id_type=MESH)
    pl.semaphore_signal(barrier, inc=1, device_id=sib, device_id_type=MESH)

    def load_v(j):
        for p in range(2):
            for i in range(I):
                pltpu.make_async_copy(
                    v.at[p, i, j], vs.at[j, pl.ds((p * I + i) * K, K)], v_sem.at[j]).start()

    loop(J, load_v)
    for i in range(I):
        for p in range(2):
            pltpu.make_async_copy(u.at[p * I + i], us.at[i, pl.ds(p * JK, JK)], u_sem.at[i]).start()
    pl.semaphore_wait(barrier, R + C - 1)

    def xg(e, q, r2):
        reg = xs.at[e, jds(q), tds(r, h)]
        return rc(reg, reg, xg_s.at[e, q, r2], xg_r.at[e, q, r], {"row": r2})

    def xg_in(e, q, r2):
        reg = xs.at[e, jds(q), tds(r2, h)]
        return rc(reg, reg, xg_s.at[e, q, r2], xg_r.at[e, q, r2], {"row": r2})

    def xf(e, q, r2):
        reg = xs.at[e, jds(q), tds(r2, h)]
        return rc(reg, reg, xf_s.at[e, q, r2], xf_r.at[e, q, r2], sib)

    def xf_in(e, q, r2):
        reg = xs.at[e, jds(q), tds(r2, 1 - h)]
        return rc(reg, reg, xf_s.at[e, q, r2], xf_r.at[e, q, r2], sib)

    def send_x(e, q):
        if e == 0:
            x_load(q).wait()
        a, b = xin[0, jds(q)].astype(F32), xin[1, jds(q)].astype(F32)
        xs[e, jds(q), tds(r, h)] = split(e, a, b).astype(BF)
        for d in range(1, R):
            xg(e, q, row(d)).start()
        xf(e, q, r).start()

    for e in range(2):
        loop(NC, functools.partial(send_x, e))

    kio = lax.broadcasted_iota(jnp.int32, (K, N), 0) + h * K

    def keep(i, j, value):
        return jnp.where(kio < ranks[i, j], value, 0.0)

    def coef(e, j):
        if e == 0:
            pltpu.make_async_copy(vs.at[j], vs.at[j], v_sem.at[j]).wait()
        m = jnp.dot(vs[j], xs[e, j], preferred_element_type=F32)
        y = m[:IK] + turn(m[IK:])
        for i in range(I):
            cf[e, i, pl.ds(pl.multiple_of(j * K, 8), K)] = keep(i, j, y[i * K:(i + 1) * K])

    def x_pass(e, q):
        for d in range(1, R):
            xg_in(e, q, row(d)).wait_recv()
            xf(e, q, row(d)).start()

    def coefs(e, q):
        for r2 in range(R):
            xf_in(e, q, r2).wait_recv()
        loop(JC, lambda jj: coef(e, q * JC + jj))

    def pair(y):
        return jnp.concatenate([y.astype(BF), (-turn(y)).astype(BF)], axis=0)

    def fs(e, i):
        return rc(fss.at[e, i], fsr.at[e, i], fs_s.at[e, i], fs_r.at[e, i], sib)

    def zc(e, i, c2):
        return rc(zs.at[e, i, c2], zr.at[e, i, c], z_s.at[e, i, c2], z_r.at[e, i, c], {"col": c2})

    def zc_in(e, i, c2):
        return rc(zs.at[e, i, c2], zr.at[e, i, c2], z_s.at[e, i, c2], z_r.at[e, i, c2], {"col": c2})

    def forward(e, i):
        if e == 0:
            pltpu.make_async_copy(us.at[i], us.at[i], u_sem.at[i]).wait()
        ft[...] = mul_t(us[i], pair(cf[e, i]))
        for c2 in range(C):
            fo[e, i, pl.ds(c2 * SB, SB)] = ft[sds(c2, h)]
            fss[e, i, pl.ds(c2 * SB, SB)] = ft[sds(c2, 1 - h)].astype(BF)
        fs(e, i).start()

    def z_send(e, i):
        fs(e, i).wait_recv()
        for d in range(1, C):
            c2 = col(d)
            zs[e, i, c2] = (fo[e, i, sblk(c2)] + fsr[e, i, sblk(c2)].astype(F32)).astype(BF)
            zc(e, i, c2).start()

    def rg(e, i, c2):
        reg = rs.at[e, i, sds(c, h)]
        return rc(reg, reg, rg_s.at[e, i, c2], rg_r.at[e, i, c], {"col": c2})

    def rg_in(e, i, c2):
        reg = rs.at[e, i, sds(c2, h)]
        return rc(reg, reg, rg_s.at[e, i, c2], rg_r.at[e, i, c2], {"col": c2})

    def rf(e, i, c2):
        reg = rs.at[e, i, sds(c2, h)]
        return rc(reg, reg, rf_s.at[e, i, c2], rf_r.at[e, i, c2], sib)

    def rf_in(e, i, c2):
        reg = rs.at[e, i, sds(c2, 1 - h)]
        return rc(reg, reg, rf_s.at[e, i, c2], rf_r.at[e, i, c2], sib)

    def resid(e, i):
        tot = fo[e, i, sblk(c)] + fsr[e, i, sblk(c)].astype(F32)
        for d in range(1, C):
            zc_in(e, i, col(d)).wait_recv()
            tot = tot + zr[e, i, col(d)].astype(F32)
        w = amp[i].astype(F32)
        o = split(e, obs[0, i].astype(F32), obs[1, i].astype(F32))
        rs[e, i, sds(c, h)] = (split(e, w, w) * (tot - o)).astype(BF)
        for d in range(1, C):
            rg(e, i, col(d)).start()
        rf(e, i, c).start()

    def r_pass(e, i):
        for d in range(1, C):
            rg_in(e, i, col(d)).wait_recv()
            rf(e, i, col(d)).start()

    def res_out(i):
        a, b = rs[0, i, sds(c, h)].astype(F32), rs[1, i, sds(c, h)].astype(F32)
        res_o[0, i] = split(0, a, b).astype(BF)
        res_o[1, i] = split(1, a, b).astype(BF)

    def back(e, i):
        for c2 in range(C):
            rf_in(e, i, c2).wait_recv()
        m = jnp.dot(us[i], rs[e, i], preferred_element_type=F32)
        cf[e, i] = m[:JK] + turn(m[JK:])

    def asx(e, q):
        return rc(ass.at[e, jds(q)], asr.at[e, jds(q)], as_s.at[e, q], as_r.at[e, q], sib)

    def ag(e, q, r2):
        return rc(gs.at[e, q, r2], gr.at[e, q, r], ag_s.at[e, q, r2], ag_r.at[e, q, r], {"row": r2})

    def ag_in(e, q, r2):
        return rc(gs.at[e, q, r2], gr.at[e, q, r2], ag_s.at[e, q, r2], ag_r.at[e, q, r2], {"row": r2})

    def adjoint(e, j):
        y = jnp.concatenate(
            [keep(i, j, cf[e, i, pl.ds(pl.multiple_of(j * K, 8), K)]) for i in range(I)], axis=0)
        at[...] = mul_t(vs[j], pair(y))
        for r2 in range(R):
            ao[e, j, pl.ds(r2 * TB, TB)] = at[tds(r2, h)]
            ass[e, j, pl.ds(r2 * TB, TB)] = at[tds(r2, 1 - h)].astype(BF)

    def adjoints(e, q):
        loop(JC, lambda jj: adjoint(e, q * JC + jj))
        asx(e, q).start()

    def a_send(e, q):
        asx(e, q).wait_recv()
        for d in range(1, R):
            r2 = row(d)
            gs[e, q, r2] = (ao[e, jds(q), tblk(r2)] + asr[e, jds(q), tblk(r2)].astype(F32)).astype(BF)
            ag(e, q, r2).start()

    def a_sum(e, q):
        tot = ao[e, jds(q), tblk(r)] + asr[e, jds(q), tblk(r)].astype(F32)
        for d in range(1, R):
            ag_in(e, q, row(d)).wait_recv()
            tot = tot + gr[e, q, row(d)].astype(F32)
        return tot

    def final(q):
        a, b = a_sum(0, q), a_sum(1, q)
        adj_o[0, jds(q)] = split(0, a, b).astype(BF)
        adj_o[1, jds(q)] = split(1, a, b).astype(BF)

    def stages(*items):
        def step(s):
            for count, delay, f in items:
                @pl.when((s >= delay) & (s < count + delay))
                def _():
                    f(s - delay)

        loop(max(count + delay for count, delay, _ in items), step)

    at_half = functools.partial
    stages((NC, 0, at_half(x_pass, 0)), (NC, 1, at_half(coefs, 0)))
    stages((I, 0, at_half(forward, 0)), (I, 1, at_half(z_send, 0)))
    stages((NC, 0, at_half(x_pass, 1)), (NC, 1, at_half(coefs, 1)), (I, 0, at_half(resid, 0)))
    stages((I, 0, at_half(forward, 1)), (I, 1, at_half(z_send, 1)), (I, 0, at_half(r_pass, 0)))
    loop(I, at_half(back, 0))
    stages((NC, 0, at_half(adjoints, 0)), (NC, 1, at_half(a_send, 0)), (I, 0, at_half(resid, 1)))
    loop(I, at_half(r_pass, 1))
    loop(I, res_out)
    loop(I, at_half(back, 1))
    stages((NC, 0, at_half(adjoints, 1)), (NC, 1, at_half(a_send, 1)))
    loop(NC, final)

    def drain_q(q):
        for e in range(2):
            for d in range(1, R):
                xg(e, q, row(d)).wait_send()
                ag(e, q, row(d)).wait_send()
            for d in range(R):
                xf(e, q, row(d)).wait_send()
            asx(e, q).wait_send()

    loop(NC, drain_q)

    def drain_i(i):
        for e in range(2):
            fs(e, i).wait_send()
            for d in range(1, C):
                zc(e, i, col(d)).wait_send()
                rg(e, i, col(d)).wait_send()
            for d in range(C):
                rf(e, i, col(d)).wait_send()

    loop(I, drain_i)


def body(R, C, wavefield, basis_factor, second_factor, tile_ranks, observed, amplitude):
    _, J, TB, N = wavefield.shape
    _, I, _, K, S = basis_factor.shape
    T = second_factor.shape[4]
    SB = observed.shape[2]
    JC = 4 if J % 4 == 0 else 1
    NC = J // JC
    vm = pltpu.VMEM
    dma = pltpu.SemaphoreType.DMA
    anys = pl.BlockSpec(memory_space=pl.ANY)
    vmem = pl.BlockSpec(memory_space=pltpu.VMEM)
    smem = pl.BlockSpec(memory_space=pltpu.SMEM)
    u = basis_factor.reshape(2 * I, J * K, S)
    return pl.pallas_call(
        functools.partial(kernel, R, C, JC),
        out_shape=(
            jax.ShapeDtypeStruct((2, I, SB, N), BF),
            jax.ShapeDtypeStruct((2, J, TB, N), BF),
        ),
        in_specs=[anys, anys, anys, smem, vmem, vmem],
        out_specs=(vmem, vmem),
        scratch_shapes=[
            vm((I, 2 * J * K, S), BF),
            vm((J, 2 * I * K, T), BF),
            vm((2, J, TB, N), BF),
            vm((2, J, T, N), BF),
            vm((2, I, J * K, N), F32),
            vm((S, N), F32),
            vm((2, I, C * SB, N), F32),
            vm((2, I, C * SB, N), BF),
            vm((2, I, C * SB, N), BF),
            vm((2, I, C, SB, N), BF),
            vm((2, I, C, SB, N), BF),
            vm((2, I, S, N), BF),
            vm((T, N), F32),
            vm((2, J, R * TB, N), F32),
            vm((2, J, R * TB, N), BF),
            vm((2, J, R * TB, N), BF),
            vm((2, NC, R, JC, TB, N), BF),
            vm((2, NC, R, JC, TB, N), BF),
            dma((I,)), dma((J,)), dma((NC,)),
            dma((2, NC, R)), dma((2, NC, R)), dma((2, NC, R)), dma((2, NC, R)),
            dma((2, I)), dma((2, I)), dma((2, I, C)), dma((2, I, C)),
            dma((2, I, C)), dma((2, I, C)), dma((2, I, C)), dma((2, I, C)),
            dma((2, NC)), dma((2, NC)), dma((2, NC, R)), dma((2, NC, R)),
        ],
        compiler_params=pltpu.CompilerParams(
            collective_id=0, has_side_effects=True, vmem_limit_bytes=60 * 1024 * 1024),
        name="mdc",
    )(wavefield, u, second_factor, tile_ranks, observed, amplitude)


def solution(mesh):
    return jax.shard_map(
        functools.partial(body, mesh.shape["row"], mesh.shape["col"]),
        mesh=mesh,
        in_specs=(
            P("freq", "col", ("row", "help"), None),
            P("freq", "row", "col", "help", None),
            P("freq", "row", "col", "help", None),
            P(("freq", "row"), "col"),
            P("freq", "row", ("col", "help"), None),
            P(("freq", "row"), ("col", "help"), None),
        ),
        out_specs=(
            P("freq", "row", ("col", "help"), None),
            P("freq", "col", ("row", "help"), None),
        ),
        check_vma=False,
    )
```

```python
import functools

import jax
import jax.numpy as jnp
from jax import lax
from jax.experimental import pallas as pl
from jax.experimental.pallas import tpu as pltpu
from jax.sharding import PartitionSpec as P

MESH = pl.DeviceIdType.MESH
BF, F32 = jnp.bfloat16, jnp.float32


def loop(n, f):
    def step(i, carry):
        f(i)
        return carry

    lax.fori_loop(0, n, step, 0)


def kernel(R, C, JC, x, u, v, ranks_h, obs_h, amp_h, res_o, adj_o,
           us, vs, xin, xs, cf, ft, fo, fss, fsr, zs, zr, rs, at, ao, ass, asr, gs, gr,
           ut, vt, u_sem, v_sem, x_sem, xg_s, xg_r, xf_s, xf_r, fs_s, fs_r, z_s, z_r,
           rg_s, rg_r, rf_s, rf_r, as_s, as_r, ag_s, ag_r, res_v, adj_v, ro_sem, ao_sem,
           ranks, obs, amp, d_sem):
    _, J, TB, N = x.shape
    I, SB = obs.shape[1], obs.shape[2]
    K = v.shape[3]
    IK, JK = I * K, J * K
    NC = J // JC
    n = N // 2
    r, c, h = lax.axis_index("row"), lax.axis_index("col"), lax.axis_index("help")
    sib = {"help": 1 - h}

    def row(d):
        return lax.rem(r + d, R)

    def col(d):
        return lax.rem(c + d, C)

    def tds(r2, h2):
        return pl.ds(pl.multiple_of((r2 * 2 + h2) * TB, TB), TB)

    def sds(c2, h2):
        return pl.ds(pl.multiple_of((c2 * 2 + h2) * SB, SB), SB)

    def sblk(c2):
        return pl.ds(pl.multiple_of(c2 * SB, SB), SB)

    def tblk(r2):
        return pl.ds(pl.multiple_of(r2 * TB, TB), TB)

    def jds(q):
        return pl.ds(q * JC, JC)

    def rc(src, dst, s, rr, dev):
        return pltpu.make_async_remote_copy(
            src_ref=src, dst_ref=dst, send_sem=s, recv_sem=rr, device_id=dev, device_id_type=MESH)

    def swap(y):
        return pltpu.roll(y, n, y.ndim - 1)

    def low(y):
        return lax.broadcasted_iota(jnp.int32, y.shape, y.ndim - 1) < n

    def split(e, a, b):
        return jnp.where(low(a), a, swap(b)) if e == 0 else jnp.where(low(a), swap(a), b)

    def turn(y):
        z = swap(y)
        return jnp.where(low(y), z, -z)

    def x_load(q):
        return pltpu.make_async_copy(x.at[:, jds(q)], xin.at[:, jds(q)], x_sem.at[q])

    loop(NC, lambda q: x_load(q).start())
    small = [pltpu.make_async_copy(a, b, d_sem.at[k]) for k, (a, b) in enumerate(
        ((ranks_h, ranks), (obs_h, obs), (amp_h, amp)))]

    barrier = pltpu.get_barrier_semaphore()
    for d in range(1, R):
        pl.semaphore_signal(barrier, inc=1, device_id={"row": row(d)}, device_id_type=MESH)
    for d in range(1, C):
        pl.semaphore_signal(barrier, inc=1, device_id={"col": col(d)}, device_id_type=MESH)
    pl.semaphore_signal(barrier, inc=1, device_id=sib, device_id_type=MESH)

    def load_v(j):
        for p in range(2):
            for i in range(I):
                pltpu.make_async_copy(
                    v.at[p, i, j], vs.at[j, pl.ds((p * I + i) * K, K)], v_sem.at[j]).start()

    def load_u(i):
        for p in range(2):
            pltpu.make_async_copy(u.at[p * I + i], us.at[i, pl.ds(p * JK, JK)], u_sem.at[i]).start()

    def xg(e, q, r2):
        reg = xs.at[e, jds(q), tds(r, h)]
        return rc(reg, reg, xg_s.at[e, q, r2], xg_r.at[e, q, r], {"row": r2})

    def xg_in(e, q, r2):
        reg = xs.at[e, jds(q), tds(r2, h)]
        return rc(reg, reg, xg_s.at[e, q, r2], xg_r.at[e, q, r2], {"row": r2})

    def xf(e, q, r2):
        reg = xs.at[e, jds(q), tds(r2, h)]
        return rc(reg, reg, xf_s.at[e, q, r2], xf_r.at[e, q, r2], sib)

    def xf_in(e, q, r2):
        reg = xs.at[e, jds(q), tds(r2, 1 - h)]
        return rc(reg, reg, xf_s.at[e, q, r2], xf_r.at[e, q, r2], sib)

    def pack_x(e, q):
        if e == 0:
            x_load(q).wait()
        a, b = xin[0, jds(q)].astype(F32), xin[1, jds(q)].astype(F32)
        xs[e, jds(q), tds(r, h)] = split(e, a, b).astype(BF)

    def send_x(e, q):
        for d in range(1, R):
            xg(e, q, row(d)).start()
        xf(e, q, r).start()

    for e in range(2):
        loop(NC, functools.partial(pack_x, e))
        if e == 0:
            pl.semaphore_wait(barrier, R + C - 1)
        if e == 0:
            loop(NC, functools.partial(send_x, 0))
            small[0].start()
            loop(J, load_v)
    loop(I, load_u)
    small[1].start()
    small[2].start()
    small[0].wait()

    kio = lax.broadcasted_iota(jnp.int32, (K, N), 0) + h * K

    def keep(i, j, value):
        return jnp.where(kio < ranks[i, j], value, 0.0)

    def coef(e, j):
        if e == 0:
            pltpu.make_async_copy(vs.at[j], vs.at[j], v_sem.at[j]).wait()
            vt[j] = vs[j].T
        m = jnp.dot(vs[j], xs[e, j], preferred_element_type=F32)
        y = m[:IK] + turn(m[IK:])
        for i in range(I):
            cf[e, i, pl.ds(pl.multiple_of(j * K, 8), K)] = keep(i, j, y[i * K:(i + 1) * K])

    def x_pass(e, q):
        for d in range(1, R):
            xg_in(e, q, row(d)).wait_recv()
            xf(e, q, row(d)).start()

    def coefs(e, q):
        for r2 in range(R):
            xf_in(e, q, r2).wait_recv()
        loop(JC, lambda jj: coef(e, q * JC + jj))

    def pair(y):
        return jnp.concatenate([y.astype(BF), (-turn(y)).astype(BF)], axis=0)

    def fs(e, i):
        return rc(fss.at[e, i], fsr.at[e, i], fs_s.at[e, i], fs_r.at[e, i], sib)

    def zc(e, i, c2):
        return rc(zs.at[e, i, c2], zr.at[e, i, c], z_s.at[e, i, c2], z_r.at[e, i, c], {"col": c2})

    def zc_in(e, i, c2):
        return rc(zs.at[e, i, c2], zr.at[e, i, c2], z_s.at[e, i, c2], z_r.at[e, i, c2], {"col": c2})

    def turn_u(i):
        pltpu.make_async_copy(us.at[i], us.at[i], u_sem.at[i]).wait()
        ut[i] = us[i].T

    def forward(e, i):
        ft[...] = jnp.dot(ut[i], pair(cf[e, i]), preferred_element_type=F32)
        for c2 in range(C):
            fo[e, i, pl.ds(c2 * SB, SB)] = ft[sds(c2, h)]
            fss[e, i, pl.ds(c2 * SB, SB)] = ft[sds(c2, 1 - h)].astype(BF)
        fs(e, i).start()

    def z_send(e, i):
        fs(e, i).wait_recv()
        for d in range(1, C):
            c2 = col(d)
            zs[e, i, c2] = (fo[e, i, sblk(c2)] + fsr[e, i, sblk(c2)].astype(F32)).astype(BF)
            zc(e, i, c2).start()

    def rg(e, i, c2):
        reg = rs.at[e, i, sds(c, h)]
        return rc(reg, reg, rg_s.at[e, i, c2], rg_r.at[e, i, c], {"col": c2})

    def rg_in(e, i, c2):
        reg = rs.at[e, i, sds(c2, h)]
        return rc(reg, reg, rg_s.at[e, i, c2], rg_r.at[e, i, c2], {"col": c2})

    def rf(e, i, c2):
        reg = rs.at[e, i, sds(c2, h)]
        return rc(reg, reg, rf_s.at[e, i, c2], rf_r.at[e, i, c2], sib)

    def rf_in(e, i, c2):
        reg = rs.at[e, i, sds(c2, 1 - h)]
        return rc(reg, reg, rf_s.at[e, i, c2], rf_r.at[e, i, c2], sib)

    def resid(e, i):
        tot = fo[e, i, sblk(c)] + fsr[e, i, sblk(c)].astype(F32)
        for d in range(1, C):
            zc_in(e, i, col(d)).wait_recv()
            tot = tot + zr[e, i, col(d)].astype(F32)
        w = amp[i].astype(F32)
        o = split(e, obs[0, i].astype(F32), obs[1, i].astype(F32))
        rs[e, i, sds(c, h)] = (split(e, w, w) * (tot - o)).astype(BF)
        for d in range(1, C):
            rg(e, i, col(d)).start()
        rf(e, i, c).start()

    def r_pass(e, i):
        for d in range(1, C):
            rg_in(e, i, col(d)).wait_recv()
            rf(e, i, col(d)).start()

    def res_put(i):
        return pltpu.make_async_copy(res_v.at[:, i], res_o.at[:, i], ro_sem.at[i])

    def adj_put(q):
        return pltpu.make_async_copy(adj_v.at[:, jds(q)], adj_o.at[:, jds(q)], ao_sem.at[q])

    def res_out(i):
        a, b = rs[0, i, sds(c, h)].astype(F32), rs[1, i, sds(c, h)].astype(F32)
        res_v[0, i] = split(0, a, b).astype(BF)
        res_v[1, i] = split(1, a, b).astype(BF)
        res_put(i).start()

    def back(e, i):
        for c2 in range(C):
            rf_in(e, i, c2).wait_recv()
        m = jnp.dot(us[i], rs[e, i], preferred_element_type=F32)
        cf[e, i] = m[:JK] + turn(m[JK:])

    def asx(e, q):
        return rc(ass.at[e, jds(q)], asr.at[e, jds(q)], as_s.at[e, q], as_r.at[e, q], sib)

    def ag(e, q, r2):
        return rc(gs.at[e, q, r2], gr.at[e, q, r], ag_s.at[e, q, r2], ag_r.at[e, q, r], {"row": r2})

    def ag_in(e, q, r2):
        return rc(gs.at[e, q, r2], gr.at[e, q, r2], ag_s.at[e, q, r2], ag_r.at[e, q, r2], {"row": r2})

    def adjoint(e, j):
        y = jnp.concatenate(
            [keep(i, j, cf[e, i, pl.ds(pl.multiple_of(j * K, 8), K)]) for i in range(I)], axis=0)
        at[...] = jnp.dot(vt[j], pair(y), preferred_element_type=F32)
        for r2 in range(R):
            ao[e, j, pl.ds(r2 * TB, TB)] = at[tds(r2, h)]
            ass[e, j, pl.ds(r2 * TB, TB)] = at[tds(r2, 1 - h)].astype(BF)

    def adjoints(e, q):
        loop(JC, lambda jj: adjoint(e, q * JC + jj))
        asx(e, q).start()

    def a_send(e, q):
        asx(e, q).wait_recv()
        for d in range(1, R):
            r2 = row(d)
            gs[e, q, r2] = (ao[e, jds(q), tblk(r2)] + asr[e, jds(q), tblk(r2)].astype(F32)).astype(BF)
            ag(e, q, r2).start()

    def a_sum(e, q):
        tot = ao[e, jds(q), tblk(r)] + asr[e, jds(q), tblk(r)].astype(F32)
        for d in range(1, R):
            ag_in(e, q, row(d)).wait_recv()
            tot = tot + gr[e, q, row(d)].astype(F32)
        return tot

    def final(q):
        a, b = a_sum(0, q), a_sum(1, q)
        adj_v[0, jds(q)] = split(0, a, b).astype(BF)
        adj_v[1, jds(q)] = split(1, a, b).astype(BF)
        adj_put(q).start()

    def stages(*items):
        def step(s):
            for count, delay, f in items:
                @pl.when((s >= delay) & (s < count + delay))
                def _():
                    f(s - delay)

        loop(max(count + delay for count, delay, _ in items), step)

    at_half = functools.partial
    lag = NC // 4
    small[1].wait()
    small[2].wait()
    stages((NC, 0, at_half(x_pass, 0)), (NC, 0, at_half(send_x, 1)), (NC, 1, at_half(coefs, 0)),
           (I, 2, turn_u))
    stages((I, 0, at_half(forward, 0)), (I, 1, at_half(z_send, 0)))
    stages((NC, 0, at_half(x_pass, 1)), (NC, 1, at_half(coefs, 1)),
           (I, lag, at_half(resid, 0)), (I, 2 * lag + 1, at_half(r_pass, 0)))
    stages((I, 0, at_half(forward, 1)), (I, 1, at_half(z_send, 1)), (I, 0, at_half(back, 0)))
    stages((NC, 0, at_half(adjoints, 0)), (NC, 1, at_half(a_send, 0)),
           (I, lag, at_half(resid, 1)), (I, 3 * lag, at_half(r_pass, 1)))
    loop(I, res_out)
    loop(I, at_half(back, 1))
    stages((NC, 0, at_half(adjoints, 1)), (NC, 1, at_half(a_send, 1)))
    loop(NC, final)

    def drain_q(q):
        adj_put(q).wait()
        for e in range(2):
            for d in range(1, R):
                xg(e, q, row(d)).wait_send()
                ag(e, q, row(d)).wait_send()
            for d in range(R):
                xf(e, q, row(d)).wait_send()
            asx(e, q).wait_send()

    loop(NC, drain_q)

    def drain_i(i):
        res_put(i).wait()
        for e in range(2):
            fs(e, i).wait_send()
            for d in range(1, C):
                zc(e, i, col(d)).wait_send()
                rg(e, i, col(d)).wait_send()
            for d in range(C):
                rf(e, i, col(d)).wait_send()

    loop(I, drain_i)


def hand_over(res, adj, res_o, adj_o, res_v, adj_v, in_sem, out_sem):
    parts = ((adj.at[0], adj_v.at[0], adj_o.at[0]), (adj.at[1], adj_v.at[1], adj_o.at[1]), (res, res_v, res_o))
    ins = [pltpu.make_async_copy(a, b, in_sem.at[k]) for k, (a, b, _) in enumerate(parts)]
    outs = [pltpu.make_async_copy(b, a, out_sem.at[k]) for k, (_, b, a) in enumerate(parts)]
    for copy in ins:
        copy.start()
    for arrive, leave in zip(ins, outs):
        arrive.wait()
        leave.start()
    for copy in outs:
        copy.wait()


def body(R, C, wavefield, basis_factor, second_factor, tile_ranks, observed, amplitude):
    _, J, TB, N = wavefield.shape
    _, I, _, K, S = basis_factor.shape
    T = second_factor.shape[4]
    SB = observed.shape[2]
    JC = 2 if J % 2 == 0 else 1
    NC = J // JC
    vm = pltpu.VMEM
    dma = pltpu.SemaphoreType.DMA
    anys = pl.BlockSpec(memory_space=pl.ANY)
    u = basis_factor.reshape(2 * I, J * K, S)
    sums = pl.pallas_call(
        functools.partial(kernel, R, C, JC),
        out_shape=(
            jax.ShapeDtypeStruct((2, I, SB, N), BF),
            jax.ShapeDtypeStruct((2, J, TB, N), BF),
        ),
        in_specs=[anys] * 6,
        out_specs=(anys, anys),
        scratch_shapes=[
            vm((I, 2 * J * K, S), BF),
            vm((J, 2 * I * K, T), BF),
            vm((2, J, TB, N), BF),
            vm((2, J, T, N), BF),
            vm((2, I, J * K, N), F32),
            vm((S, N), F32),
            vm((2, I, C * SB, N), F32),
            vm((2, I, C * SB, N), BF),
            vm((2, I, C * SB, N), BF),
            vm((2, I, C, SB, N), BF),
            vm((2, I, C, SB, N), BF),
            vm((2, I, S, N), BF),
            vm((T, N), F32),
            vm((2, J, R * TB, N), F32),
            vm((2, J, R * TB, N), BF),
            vm((2, J, R * TB, N), BF),
            vm((2, NC, R, JC, TB, N), BF),
            vm((2, NC, R, JC, TB, N), BF),
            vm((I, S, 2 * J * K), BF), vm((J, T, 2 * I * K), BF),
            dma((I,)), dma((J,)), dma((NC,)),
            dma((2, NC, R)), dma((2, NC, R)), dma((2, NC, R)), dma((2, NC, R)),
            dma((2, I)), dma((2, I)), dma((2, I, C)), dma((2, I, C)),
            dma((2, I, C)), dma((2, I, C)), dma((2, I, C)), dma((2, I, C)),
            dma((2, NC)), dma((2, NC)), dma((2, NC, R)), dma((2, NC, R)),
            vm((2, I, SB, N), BF), vm((2, J, TB, N), BF), dma((I,)), dma((NC,)),
            pltpu.SMEM(tile_ranks.shape, jnp.int32), vm(observed.shape, BF), vm(amplitude.shape, BF), dma((3,)),
        ],
        compiler_params=pltpu.CompilerParams(
            collective_id=0, has_side_effects=True, vmem_limit_bytes=60 * 1024 * 1024),
        name="mdc",
    )(wavefield, u, second_factor, tile_ranks, observed, amplitude)
    return pl.pallas_call(
        hand_over,
        out_shape=tuple(jax.ShapeDtypeStruct(y.shape, y.dtype) for y in sums),
        in_specs=[anys, anys],
        out_specs=(anys, anys),
        scratch_shapes=[vm(y.shape, y.dtype) for y in sums] + [dma((3,)), dma((3,))],
        name="out",
    )(*sums)


def solution(mesh):
    return jax.shard_map(
        functools.partial(body, mesh.shape["row"], mesh.shape["col"]),
        mesh=mesh,
        in_specs=(
            P("freq", "col", ("row", "help"), None),
            P("freq", "row", "col", "help", None),
            P("freq", "row", "col", "help", None),
            P(("freq", "row"), "col"),
            P("freq", "row", ("col", "help"), None),
            P(("freq", "row"), ("col", "help"), None),
        ),
        out_specs=(
            P("freq", "row", ("col", "help"), None),
            P("freq", "col", ("row", "help"), None),
        ),
        check_vma=False,
    )
```

```python
import functools

import jax
import jax.numpy as jnp
from jax import lax
from jax.experimental import pallas as pl
from jax.experimental.pallas import tpu as pltpu
from jax.sharding import PartitionSpec as P

MESH = pl.DeviceIdType.MESH
BF, F32 = jnp.bfloat16, jnp.float32


def loop(n, f):
    def step(i, carry):
        f(i)
        return carry

    lax.fori_loop(0, n, step, 0)


def kernel(R, C, JC, x, u, v, ranks_h, obs_h, amp_h, res_o, adj_o,
           us, vs, xin, xs, cf, ft, fo, fss, fsr, zs, zr, rs, at, ao, ass, asr, gs, gr,
           ut, vt, u_sem, v_sem, x_sem, xg_s, xg_r, xf_s, xf_r, fs_s, fs_r, z_s, z_r,
           rg_s, rg_r, rf_s, rf_r, as_s, as_r, ag_s, ag_r, res_v, adj_v, ro_sem, ao_sem,
           ranks, obs, amp, d_sem):
    _, J, TB, N = x.shape
    I, SB = obs.shape[1], obs.shape[2]
    K = v.shape[3]
    IK, JK = I * K, J * K
    NC = J // JC
    n = N // 2
    r, c, h = lax.axis_index("row"), lax.axis_index("col"), lax.axis_index("help")
    sib = {"help": 1 - h}

    def row(d):
        return lax.rem(r + d, R)

    def col(d):
        return lax.rem(c + d, C)

    def tds(r2, h2):
        return pl.ds(pl.multiple_of((r2 * 2 + h2) * TB, TB), TB)

    def sds(c2, h2):
        return pl.ds(pl.multiple_of((c2 * 2 + h2) * SB, SB), SB)

    def sblk(c2):
        return pl.ds(pl.multiple_of(c2 * SB, SB), SB)

    def tblk(r2):
        return pl.ds(pl.multiple_of(r2 * TB, TB), TB)

    def jds(q):
        return pl.ds(q * JC, JC)

    def rc(src, dst, s, rr, dev):
        return pltpu.make_async_remote_copy(
            src_ref=src, dst_ref=dst, send_sem=s, recv_sem=rr, device_id=dev, device_id_type=MESH)

    def swap(y):
        return pltpu.roll(y, n, y.ndim - 1)

    def low(y):
        return lax.broadcasted_iota(jnp.int32, y.shape, y.ndim - 1) < n

    def split(e, a, b):
        return jnp.where(low(a), a, swap(b)) if e == 0 else jnp.where(low(a), swap(a), b)

    def turn(y):
        z = swap(y)
        return jnp.where(low(y), z, -z)

    def x_load(q):
        return pltpu.make_async_copy(x.at[:, jds(q)], xin.at[:, jds(q)], x_sem.at[q])

    loop(NC, lambda q: x_load(q).start())
    small = [pltpu.make_async_copy(a, b, d_sem.at[k]) for k, (a, b) in enumerate(
        ((ranks_h, ranks), (obs_h, obs), (amp_h, amp)))]

    barrier = pltpu.get_barrier_semaphore()
    for d in range(1, R):
        pl.semaphore_signal(barrier, inc=1, device_id={"row": row(d)}, device_id_type=MESH)
    for d in range(1, C):
        pl.semaphore_signal(barrier, inc=1, device_id={"col": col(d)}, device_id_type=MESH)
    pl.semaphore_signal(barrier, inc=1, device_id=sib, device_id_type=MESH)

    def load_v(j):
        for p in range(2):
            for i in range(I):
                pltpu.make_async_copy(
                    v.at[p, i, j], vs.at[j, pl.ds((p * I + i) * K, K)], v_sem.at[j]).start()

    def load_u(i):
        for p in range(2):
            pltpu.make_async_copy(u.at[p * I + i], us.at[i, pl.ds(p * JK, JK)], u_sem.at[i]).start()

    def xg(e, q, r2):
        reg = xs.at[e, jds(q), tds(r, h)]
        return rc(reg, reg, xg_s.at[e, q, r2], xg_r.at[e, q, r], {"row": r2})

    def xg_in(e, q, r2):
        reg = xs.at[e, jds(q), tds(r2, h)]
        return rc(reg, reg, xg_s.at[e, q, r2], xg_r.at[e, q, r2], {"row": r2})

    def xf(e, q, r2):
        reg = xs.at[e, jds(q), tds(r2, h)]
        return rc(reg, reg, xf_s.at[e, q, r2], xf_r.at[e, q, r2], sib)

    def xf_in(e, q, r2):
        reg = xs.at[e, jds(q), tds(r2, 1 - h)]
        return rc(reg, reg, xf_s.at[e, q, r2], xf_r.at[e, q, r2], sib)

    def pack_x(e, q):
        if e == 0:
            x_load(q).wait()
        a, b = xin[0, jds(q)].astype(F32), xin[1, jds(q)].astype(F32)
        xs[e, jds(q), tds(r, h)] = split(e, a, b).astype(BF)

    def send_x(e, q):
        for d in range(1, R):
            xg(e, q, row(d)).start()
        xf(e, q, r).start()

    for e in range(2):
        loop(NC, functools.partial(pack_x, e))
        if e == 0:
            pl.semaphore_wait(barrier, R + C - 1)
        if e == 0:
            loop(NC, functools.partial(send_x, 0))
            small[0].start()
            loop(J, load_v)
    loop(I, load_u)
    small[1].start()
    small[2].start()
    small[0].wait()

    kio = lax.broadcasted_iota(jnp.int32, (K, N), 0) + h * K

    def keep(i, j, value):
        return jnp.where(kio < ranks[i, j], value, 0.0)

    def coef(e, j):
        if e == 0:
            pltpu.make_async_copy(vs.at[j], vs.at[j], v_sem.at[j]).wait()
            vt[j] = vs[j].T
        m = jnp.dot(vs[j], xs[e, j], preferred_element_type=F32)
        y = m[:IK] + turn(m[IK:])
        for i in range(I):
            cf[e, i, pl.ds(pl.multiple_of(j * K, 8), K)] = keep(i, j, y[i * K:(i + 1) * K])

    def x_pass(e, q):
        for d in range(1, R):
            xg_in(e, q, row(d)).wait_recv()
            xf(e, q, row(d)).start()

    def coefs(e, q):
        for r2 in range(R):
            xf_in(e, q, r2).wait_recv()
        loop(JC, lambda jj: coef(e, q * JC + jj))

    def pair(y):
        return jnp.concatenate([y.astype(BF), (-turn(y)).astype(BF)], axis=0)

    def fs(e, i):
        return rc(fss.at[e, i], fsr.at[e, i], fs_s.at[e, i], fs_r.at[e, i], sib)

    def zc(e, i, c2):
        return rc(zs.at[e, i, c2], zr.at[e, i, c], z_s.at[e, i, c2], z_r.at[e, i, c], {"col": c2})

    def zc_in(e, i, c2):
        return rc(zs.at[e, i, c2], zr.at[e, i, c2], z_s.at[e, i, c2], z_r.at[e, i, c2], {"col": c2})

    def turn_u(i):
        pltpu.make_async_copy(us.at[i], us.at[i], u_sem.at[i]).wait()
        ut[i] = us[i].T

    def forward(e, i):
        ft[...] = jnp.dot(ut[i], pair(cf[e, i]), preferred_element_type=F32)
        for c2 in range(C):
            fo[e, i, pl.ds(c2 * SB, SB)] = ft[sds(c2, h)]
            fss[e, i, pl.ds(c2 * SB, SB)] = ft[sds(c2, 1 - h)].astype(BF)
        fs(e, i).start()

    def z_send(e, i):
        fs(e, i).wait_recv()
        for d in range(1, C):
            c2 = col(d)
            zs[e, i, c2] = (fo[e, i, sblk(c2)] + fsr[e, i, sblk(c2)].astype(F32)).astype(BF)
            zc(e, i, c2).start()

    def rg(e, i, c2):
        reg = rs.at[e, i, sds(c, h)]
        return rc(reg, reg, rg_s.at[e, i, c2], rg_r.at[e, i, c], {"col": c2})

    def rg_in(e, i, c2):
        reg = rs.at[e, i, sds(c2, h)]
        return rc(reg, reg, rg_s.at[e, i, c2], rg_r.at[e, i, c2], {"col": c2})

    def rf(e, i, c2):
        reg = rs.at[e, i, sds(c2, h)]
        return rc(reg, reg, rf_s.at[e, i, c2], rf_r.at[e, i, c2], sib)

    def rf_in(e, i, c2):
        reg = rs.at[e, i, sds(c2, 1 - h)]
        return rc(reg, reg, rf_s.at[e, i, c2], rf_r.at[e, i, c2], sib)

    def resid(e, i):
        tot = fo[e, i, sblk(c)] + fsr[e, i, sblk(c)].astype(F32)
        for d in range(1, C):
            zc_in(e, i, col(d)).wait_recv()
            tot = tot + zr[e, i, col(d)].astype(F32)
        w = amp[i].astype(F32)
        o = split(e, obs[0, i].astype(F32), obs[1, i].astype(F32))
        rs[e, i, sds(c, h)] = (split(e, w, w) * (tot - o)).astype(BF)
        for d in range(1, C):
            rg(e, i, col(d)).start()
        rf(e, i, c).start()

    def r_pass(e, i):
        for d in range(1, C):
            rg_in(e, i, col(d)).wait_recv()
            rf(e, i, col(d)).start()

    def res_put(i):
        return pltpu.make_async_copy(res_v.at[:, i], res_o.at[:, i], ro_sem.at[i])

    def adj_put(q):
        return pltpu.make_async_copy(adj_v.at[:, jds(q)], adj_o.at[:, jds(q)], ao_sem.at[q])

    def res_out(i):
        a, b = rs[0, i, sds(c, h)].astype(F32), rs[1, i, sds(c, h)].astype(F32)
        res_v[0, i] = split(0, a, b).astype(BF)
        res_v[1, i] = split(1, a, b).astype(BF)
        res_put(i).start()

    def back(e, i):
        for c2 in range(C):
            rf_in(e, i, c2).wait_recv()
        m = jnp.dot(us[i], rs[e, i], preferred_element_type=F32)
        cf[e, i] = m[:JK] + turn(m[JK:])

    def asx(e, q):
        return rc(ass.at[e, jds(q)], asr.at[e, jds(q)], as_s.at[e, q], as_r.at[e, q], sib)

    def ag(e, q, r2):
        return rc(gs.at[e, q, r2], gr.at[e, q, r], ag_s.at[e, q, r2], ag_r.at[e, q, r], {"row": r2})

    def ag_in(e, q, r2):
        return rc(gs.at[e, q, r2], gr.at[e, q, r2], ag_s.at[e, q, r2], ag_r.at[e, q, r2], {"row": r2})

    def adjoint(e, j):
        y = jnp.concatenate(
            [keep(i, j, cf[e, i, pl.ds(pl.multiple_of(j * K, 8), K)]) for i in range(I)], axis=0)
        at[...] = jnp.dot(vt[j], pair(y), preferred_element_type=F32)
        for r2 in range(R):
            ao[e, j, pl.ds(r2 * TB, TB)] = at[tds(r2, h)]
            ass[e, j, pl.ds(r2 * TB, TB)] = at[tds(r2, 1 - h)].astype(BF)

    def adjoints(e, q):
        loop(JC, lambda jj: adjoint(e, q * JC + jj))
        asx(e, q).start()

    def a_send(e, q):
        asx(e, q).wait_recv()
        for d in range(1, R):
            r2 = row(d)
            gs[e, q, r2] = (ao[e, jds(q), tblk(r2)] + asr[e, jds(q), tblk(r2)].astype(F32)).astype(BF)
            ag(e, q, r2).start()

    def a_sum(e, q):
        tot = ao[e, jds(q), tblk(r)] + asr[e, jds(q), tblk(r)].astype(F32)
        for d in range(1, R):
            ag_in(e, q, row(d)).wait_recv()
            tot = tot + gr[e, q, row(d)].astype(F32)
        return tot

    def final(q):
        a, b = a_sum(0, q), a_sum(1, q)
        adj_v[0, jds(q)] = split(0, a, b).astype(BF)
        adj_v[1, jds(q)] = split(1, a, b).astype(BF)
        adj_put(q).start()

    def stages(*items):
        def step(s):
            for count, delay, f in items:
                @pl.when((s >= delay) & (s < count + delay))
                def _():
                    f(s - delay)

        loop(max(count + delay for count, delay, _ in items), step)

    at_half = functools.partial
    lag = NC // 4
    small[1].wait()
    small[2].wait()
    stages((NC, 0, at_half(x_pass, 0)), (NC, 0, at_half(send_x, 1)), (NC, 1, at_half(coefs, 0)),
           (I, 2, turn_u))
    stages((I, 0, at_half(forward, 0)), (I, 1, at_half(z_send, 0)))
    stages((NC, 0, at_half(x_pass, 1)), (NC, 1, at_half(coefs, 1)),
           (I, lag, at_half(resid, 0)), (I, 2 * lag + 1, at_half(r_pass, 0)))
    stages((I, 0, at_half(forward, 1)), (I, 1, at_half(z_send, 1)), (I, 0, at_half(back, 0)))
    stages((NC, 0, at_half(adjoints, 0)), (NC, 1, at_half(a_send, 0)),
           (I, lag, at_half(resid, 1)), (I, 3 * lag, at_half(r_pass, 1)))
    loop(I, at_half(back, 1))
    stages((NC, 0, at_half(adjoints, 1)), (NC, 1, at_half(a_send, 1)))
    loop(I, res_out)
    loop(NC, final)

    def drain_q(q):
        adj_put(q).wait()
        for e in range(2):
            for d in range(1, R):
                xg(e, q, row(d)).wait_send()
                ag(e, q, row(d)).wait_send()
            for d in range(R):
                xf(e, q, row(d)).wait_send()
            asx(e, q).wait_send()

    loop(NC, drain_q)

    def drain_i(i):
        res_put(i).wait()
        for e in range(2):
            fs(e, i).wait_send()
            for d in range(1, C):
                zc(e, i, col(d)).wait_send()
                rg(e, i, col(d)).wait_send()
            for d in range(C):
                rf(e, i, col(d)).wait_send()

    loop(I, drain_i)


def hand_over(res, adj, res_o, adj_o, res_v, adj_v, in_sem, out_sem):
    parts = ((adj.at[0], adj_v.at[0], adj_o.at[0]), (adj.at[1], adj_v.at[1], adj_o.at[1]), (res, res_v, res_o))
    ins = [pltpu.make_async_copy(a, b, in_sem.at[k]) for k, (a, b, _) in enumerate(parts)]
    outs = [pltpu.make_async_copy(b, a, out_sem.at[k]) for k, (_, b, a) in enumerate(parts)]
    for copy in ins:
        copy.start()
    for arrive, leave in zip(ins, outs):
        arrive.wait()
        leave.start()
    for copy in outs:
        copy.wait()


def body(R, C, wavefield, basis_factor, second_factor, tile_ranks, observed, amplitude):
    _, J, TB, N = wavefield.shape
    _, I, _, K, S = basis_factor.shape
    T = second_factor.shape[4]
    SB = observed.shape[2]
    JC = 2 if J % 2 == 0 else 1
    NC = J // JC
    vm = pltpu.VMEM
    dma = pltpu.SemaphoreType.DMA
    anys = pl.BlockSpec(memory_space=pl.ANY)
    u = basis_factor.reshape(2 * I, J * K, S)
    sums = pl.pallas_call(
        functools.partial(kernel, R, C, JC),
        out_shape=(
            jax.ShapeDtypeStruct((2, I, SB, N), BF),
            jax.ShapeDtypeStruct((2, J, TB, N), BF),
        ),
        in_specs=[anys] * 6,
        out_specs=(anys, anys),
        scratch_shapes=[
            vm((I, 2 * J * K, S), BF),
            vm((J, 2 * I * K, T), BF),
            vm((2, J, TB, N), BF),
            vm((2, J, T, N), BF),
            vm((2, I, J * K, N), F32),
            vm((S, N), F32),
            vm((2, I, C * SB, N), F32),
            vm((2, I, C * SB, N), BF),
            vm((2, I, C * SB, N), BF),
            vm((2, I, C, SB, N), BF),
            vm((2, I, C, SB, N), BF),
            vm((2, I, S, N), BF),
            vm((T, N), F32),
            vm((2, J, R * TB, N), F32),
            vm((2, J, R * TB, N), BF),
            vm((2, J, R * TB, N), BF),
            vm((2, NC, R, JC, TB, N), BF),
            vm((2, NC, R, JC, TB, N), BF),
            vm((I, S, 2 * J * K), BF), vm((J, T, 2 * I * K), BF),
            dma((I,)), dma((J,)), dma((NC,)),
            dma((2, NC, R)), dma((2, NC, R)), dma((2, NC, R)), dma((2, NC, R)),
            dma((2, I)), dma((2, I)), dma((2, I, C)), dma((2, I, C)),
            dma((2, I, C)), dma((2, I, C)), dma((2, I, C)), dma((2, I, C)),
            dma((2, NC)), dma((2, NC)), dma((2, NC, R)), dma((2, NC, R)),
            vm((2, I, SB, N), BF), vm((2, J, TB, N), BF), dma((I,)), dma((NC,)),
            pltpu.SMEM(tile_ranks.shape, jnp.int32), vm(observed.shape, BF), vm(amplitude.shape, BF), dma((3,)),
        ],
        compiler_params=pltpu.CompilerParams(
            collective_id=0, has_side_effects=True, vmem_limit_bytes=60 * 1024 * 1024),
        name="mdc",
    )(wavefield, u, second_factor, tile_ranks, observed, amplitude)
    return pl.pallas_call(
        hand_over,
        out_shape=tuple(jax.ShapeDtypeStruct(y.shape, y.dtype) for y in sums),
        in_specs=[anys, anys],
        out_specs=(anys, anys),
        scratch_shapes=[vm(y.shape, y.dtype) for y in sums] + [dma((3,)), dma((3,))],
        name="out",
    )(*sums)


def solution(mesh):
    return jax.shard_map(
        functools.partial(body, mesh.shape["row"], mesh.shape["col"]),
        mesh=mesh,
        in_specs=(
            P("freq", "col", ("row", "help"), None),
            P("freq", "row", "col", "help", None),
            P("freq", "row", "col", "help", None),
            P(("freq", "row"), "col"),
            P("freq", "row", ("col", "help"), None),
            P(("freq", "row"), ("col", "help"), None),
        ),
        out_specs=(
            P("freq", "row", ("col", "help"), None),
            P("freq", "col", ("row", "help"), None),
        ),
        check_vma=False,
    )
```
